32 devices in a mesh: pb: 4 (over z), row: 4 (over y, x), col: 2 (over core).
Axes of the slice: x: 2, y: 2, z: 4, core: 2. Of those that a mesh axis runs over, the one named last changes fastest.
Arguments:
- amplitudes: bfloat16 [4, 20, 4, 9216], P('pb'), may hold values from -6 to 6
- pairs: int32 [4, 4, 2], P('pb'), may hold values from 0 to 3
- stored_k: int32 [4], replicated, may hold values from 0 to 3, each once
- orbitals: bfloat16 [4, 192, 2048], P('pb', None, ('row', 'col')), may hold values from -1.078125 to 1.078125
- valence_energy: float32 [4, 96], replicated, may hold values from -1 to 0
- conduction_energy: float32 [4, 96], replicated, may hold values from 2.5 to 3.5
- screened: bfloat16 [4, 2048, 2048], P('pb', 'row', 'col'), may hold values from -0.125 to 0.125
Outputs:
- filtered: bfloat16 [4, 20, 4, 9216], P('pb')
The draws below stay inside these ranges and needn't reach their ends.
Inputs may be any that keep to these rules, and one draw needn't show every extreme that they name: stored_k holds every k-point exactly once; row s of orbitals belongs to k-point stored_k[s]. `pairs`: each entry is a k-point.
All inputs are finite; a program needn't handle non-finite values.
Results may differ from the reference program's by a relative error of at most 0.024.
Values may be sent and summed in bfloat16 or wider, within the bound.
A program may use at most 64 MiB of HBM per device.

```python
import jax
import jax.numpy as jnp
from jax import lax

NV = 96
NC = 96
NB = 192
NP = 2048
PAIRS = 4
NVEC = 20
NQ = 4
NK = 4
N_ROW = 4
N_COL = 2


def plant(values, stream_key, smallest, top_value):
    index_at = [jax.random.randint(jax.random.fold_in(stream_key, axis), (), 0, length) for axis, length in enumerate(values.shape)]
    widest = values.shape.index(max(values.shape))
    neighbour = index_at[:widest] + [(index_at[widest] + 1) % values.shape[widest]] + index_at[widest + 1:]
    return values.at[tuple(index_at)].set(smallest).at[tuple(neighbour)].set(top_value)


def block_levels(own_key, extent, split, least, top_value):
    factor_of, own = 1.0, jax.random.fold_in(own_key, 6)
    for position, blocks in split:
        steps = jnp.exp(jax.random.uniform(jax.random.fold_in(own, position), (blocks,), jnp.float32, least / len(split), top_value / len(split)))
        factor_of = factor_of * jnp.repeat(steps, extent[position] // blocks).reshape([-1 if axis == position else 1 for axis in range(len(extent))])
    return factor_of


def centred(key, shape, deviation, bound, cuts=(), kind=jnp.bfloat16):
    result = jax.random.normal(key, shape, jnp.float32) * deviation
    if len(cuts) > 0:
        result = block_levels(key, shape, cuts, -0.22, 0.18) * result
    return jnp.clip(result, min=-bound, max=bound).astype(kind)


def setup_inputs(seed: int = 0) -> dict:
    streams_of = jax.random.split(jax.random.key(seed), 8)
    amplitudes = centred(streams_of[0], (NQ, NVEC, PAIRS, NV * NC), 1.0, 6.0, ((0, 4),))
    pairs = plant(jax.random.randint(streams_of[1], (NQ, PAIRS, 2), 0, NK), jax.random.fold_in(streams_of[1], 1), 0, NK - 1).astype(jnp.int32)
    stored_k = jax.random.permutation(streams_of[2], NK).astype(jnp.int32)
    orbitals = centred(streams_of[3], (NK, NB, NP), 0.18, 1.078125, ((0, 4), (2, 8)))
    valence_energy = jnp.clip(jax.random.uniform(streams_of[4], (NK, NV), jnp.float32, -1.0, 0.0), -1.0, 0.0)
    conduction_energy = jnp.clip(jax.random.uniform(streams_of[5], (NK, NC), jnp.float32, 2.5, 3.5), 2.5, 3.5)
    screened = centred(streams_of[6], (NQ, NP, NP), NP ** -0.5, 0.125, ((0, 4), (1, 4), (2, 2)))
    return dict(amplitudes=amplitudes, pairs=pairs, stored_k=stored_k, orbitals=orbitals, valence_energy=valence_energy, conduction_energy=conduction_energy, screened=screened)


CENTER = 3.0
HALF = 2.5


def kernel_apply(amplitude, valence, conduction_orbital, w_matrix):
    block_count = N_ROW * N_COL
    block_width = NP // block_count
    amplitude_lattice = amplitude.reshape(NVEC, PAIRS, NV, NC).astype(jnp.float32)
    inner_total_sum = jnp.einsum("iomx,oxj->iomj", amplitude_lattice, conduction_orbital.astype(jnp.float32))
    values = jnp.sum(valence.astype(jnp.float32)[None] * inner_total_sum, axis=2)
    values = values.astype(jnp.bfloat16).reshape(NVEC * PAIRS, NP)
    screened_values = jnp.dot(values, w_matrix.T, preferred_element_type=jnp.float32)
    screened_values = screened_values.reshape(NVEC, PAIRS, NP)
    weighted_product = (valence.astype(jnp.float32)[None] * screened_values[:, :, None, :]).astype(jnp.bfloat16)

    def block_sum(running, block_id):
        screened_portion = lax.dynamic_slice_in_dim(weighted_product, block_id * block_width, block_width, 3)
        conduction_portion = lax.dynamic_slice_in_dim(conduction_orbital, block_id * block_width, block_width, 2)
        block_contribution = jnp.einsum("kyqz,yhz->kyqh", screened_portion.astype(jnp.float32), conduction_portion.astype(jnp.float32))
        rounded = lax.optimization_barrier(block_contribution.astype(jnp.bfloat16))
        return running + rounded.astype(jnp.float32), None

    zeros_init = jnp.zeros((NVEC, PAIRS, NV, NC), jnp.float32)
    running, _ = lax.scan(block_sum, zeros_init, jnp.arange(block_count, dtype=jnp.int32))
    return running.reshape(NVEC, PAIRS, NV * NC)


def scaled(current, kernel_term, gap_grid):
    return (gap_grid[None] * current + kernel_term - CENTER * current) / HALF


def reference(amplitudes, pairs, stored_k, orbitals, valence_energy, conduction_energy, screened):
    inverse = jnp.zeros((NK,), jnp.int32).at[stored_k].set(jnp.arange(NK, dtype=jnp.int32))

    def per_transfer(inputs):
        amplitude, pair_list, w_matrix = inputs
        valence = orbitals[inverse[pair_list[:, 0]], :NV]
        conduction_orbital = orbitals[inverse[pair_list[:, 1]], NV:]
        low_energy = jnp.take(valence_energy, pair_list[:, 0], axis=0)
        high_energy = jnp.take(conduction_energy, pair_list[:, 1], axis=0)
        gap_grid = (high_energy[:, None, :] - low_energy[:, :, None]).reshape(PAIRS, NV * NC)
        initial = amplitude.astype(jnp.float32)
        first_term = scaled(initial, kernel_apply(amplitude, valence, conduction_orbital, w_matrix), gap_grid).astype(jnp.bfloat16)
        second_term = scaled(first_term.astype(jnp.float32), kernel_apply(first_term, valence, conduction_orbital, w_matrix), gap_grid)
        return (2.0 * second_term - initial).astype(jnp.bfloat16)

    return lax.map(per_transfer, (amplitudes, pairs, screened))
```

```python
import functools
import math

import jax
import jax.numpy as jnp
from jax import lax
from jax.experimental import pallas as pl
from jax.experimental.pallas import tpu as pltpu
from jax.sharding import PartitionSpec as P

CENTER = 3.0
HALF = 2.5
LANES = 128
MESH = pl.DeviceIdType.MESH


def dot(a, b):
    return jnp.dot(a, b, preferred_element_type=jnp.float32)


def dot_t(a, b):
    return lax.dot_general(a, b, (((1,), (1,)), ((), ())), preferred_element_type=jnp.float32)


def windows(count_c):
    group = LANES // math.gcd(count_c, LANES)
    width = group * count_c
    length = min(width, -(-count_c // LANES) * LANES + LANES)
    starts = [min(j * count_c // LANES * LANES, width - length) for j in range(group)]
    offsets = [j * count_c - starts[j] for j in range(group)]
    return group, width, length, starts, offsets


def kernel(
    sizes, pairs, stored, amp, orb, ev, ec, w, out,
    zbuf, sel, obuf, vtmp, vj, pad, mfull, mrecv, nsend, nrecv, nfull, gbuf, gap, t1,
    z_s, z_r, z_l, o_s, o_r, f_s, f_r, m_s, m_r, n_s, n_r, g_s, g_r, h_s, h_r,
):
    n_pb, n_row, n_col, count_v, count_c, vecs, points, chunks = sizes
    group, width, length, starts, offsets = windows(count_c)
    inner = count_v // group
    top = max(offsets)
    blocks = n_row * n_col
    rows_pad = mfull.shape[1]
    total = blocks * points
    half_blocks = blocks // n_col
    z, row, col = lax.axis_index("pb"), lax.axis_index("row"), lax.axis_index("col")
    me = row * n_col + col

    def peer(step):
        dr, dc = divmod(step, n_col)
        return lax.rem(row + dr, n_row), lax.rem(col + dc, n_col)

    def source(step):
        dr, dc = divmod(step, n_col)
        return lax.rem(row + n_row - dr, n_row), lax.rem(col + n_col - dc, n_col)

    def to(r, c):
        return {"row": r, "col": c}

    def remote(src, dst, send, recv, device):
        return pltpu.make_async_remote_copy(
            src_ref=src, dst_ref=dst, send_sem=send, recv_sem=recv, device_id=device, device_id_type=MESH
        )

    barrier = pltpu.get_barrier_semaphore()
    for d in range(1, n_pb):
        pl.semaphore_signal(barrier, inc=1, device_id={"pb": lax.rem(z + d, n_pb)}, device_id_type=MESH)
    for step in range(1, blocks):
        pl.semaphore_signal(barrier, inc=1, device_id=to(*peer(step)), device_id_type=MESH)
    pl.semaphore_wait(barrier, n_pb - 1 + blocks - 1)

    z_copies = []
    for d in range(1, n_pb):
        copy = remote(orb, zbuf.at[z], z_s.at[d - 1], z_r.at[d - 1], {"pb": lax.rem(z + d, n_pb)})
        copy.start()
        z_copies.append(copy)
    local = pltpu.make_async_copy(orb, zbuf.at[z], z_l)
    local.start()
    pad[...] = jnp.zeros_like(pad)
    gap[...] = ec[pairs[row, 1]] - ev[pairs[row, 0]]
    local.wait()
    for copy in z_copies:
        copy.wait()

    def find(k):
        return lax.fori_loop(0, n_pb, lambda i, s: jnp.where(stored[i] == k, i, s), jnp.int32(0))

    def pick(p):
        low, high = find(pairs[p, 0]), find(pairs[p, 1])
        return zbuf[low, :count_v, :], zbuf[high, count_v:, :]

    o_copies, f_copies = [], []
    for d in range(1, n_row):
        p = lax.rem(row + d, n_row)
        low, high = pick(p)
        sel[d - 1, :count_v] = low
        sel[d - 1, count_v:] = high
        copy = remote(sel.at[d - 1], obuf.at[me], o_s.at[d - 1], o_r.at[d - 1], to(p, col))
        copy.start()
        o_copies.append(copy)
    low, high = pick(row)
    obuf[me, :count_v] = low
    obuf[me, count_v:] = high

    def forward(d, slot):
        for e in range(1, n_col):
            copy = remote(
                obuf.at[slot], obuf.at[slot], f_s.at[e - 1, d], f_r.at[e - 1, d], to(row, lax.rem(col + e, n_col))
            )
            copy.start()
            f_copies.append((e, d, copy))

    def span(slot):
        return pl.ds(pl.multiple_of(slot * points, points), points)

    def prepare(slot):
        for t in range(points // LANES):
            vtmp[t] = obuf[slot, :count_v, t * LANES : (t + 1) * LANES].astype(jnp.float32)
            at = pl.ds(pl.multiple_of(slot * points + t * LANES, LANES), LANES)
            for j in range(group):
                vj[j, :, at] = vtmp[t, pl.ds(j, inner, stride=group), :]
        pad[top : top + count_c, span(slot)] = obuf[slot, count_v:, :]

    def expand(source_ref, slot):
        acc = None
        for j in range(group):
            value = dot(
                source_ref[:, starts[j] : starts[j] + length],
                pad[top - offsets[j] : top - offsets[j] + length, span(slot)],
            ).reshape(vecs, inner, points)
            term = value * vj[j, :, span(slot)][None]
            acc = term if acc is None else acc + term
        m = jnp.sum(acc, axis=1)
        m = jnp.concatenate([m, jnp.zeros((rows_pad - vecs, points), jnp.float32)], axis=0)
        mfull[slot] = m.astype(jnp.bfloat16)

    forward(0, me)
    prepare(me)
    expand(amp, me)
    for d in range(1, n_row):
        o_copies[d - 1].wait_recv()
        slot = lax.rem(row + n_row - d, n_row) * n_col + col
        forward(d, slot)
        prepare(slot)
        expand(amp, slot)
    for e, d, copy in f_copies:
        copy.wait_recv()
        slot = lax.rem(row + n_row - d, n_row) * n_col + lax.rem(col + n_col - e, n_col)
        prepare(slot)
        expand(amp, slot)
    for copy in o_copies:
        copy.wait_send()
    for _, _, copy in f_copies:
        copy.wait_send()

    def screen():
        copies = []
        for step in range(1, blocks):
            r, c = peer(step)
            copy = remote(
                mfull.at[pl.ds(c * half_blocks, half_blocks)], mrecv.at[me], m_s.at[step - 1], m_r.at[step - 1], to(r, c)
            )
            copy.start()
            copies.append(copy)
        mrecv[me] = mfull[pl.ds(col * half_blocks, half_blocks)]
        for copy in copies:
            copy.wait()
        partial = None
        for i in range(half_blocks):
            term = dot_t(
                mrecv[:, i].reshape(blocks * rows_pad, points), w[:, i * points : (i + 1) * points]
            )
            partial = term if partial is None else partial + term
        nsend[...] = partial.astype(jnp.bfloat16).reshape(nsend.shape)
        copies = []
        for step in range(1, blocks):
            r, c = peer(step)
            copy = remote(
                nsend.at[r * n_col + c], nrecv.at[me], n_s.at[step - 1], n_r.at[step - 1], to(r, c)
            )
            copy.start()
            copies.append(copy)
        nrecv[me] = nsend[me]
        for copy in copies:
            copy.wait()
        span_row = n_col * points
        for r in range(n_row):
            value = nrecv[r * n_col].astype(jnp.float32)
            for c in range(1, n_col):
                value = value + nrecv[r * n_col + c].astype(jnp.float32)
            nfull[:, r * span_row : (r + 1) * span_row] = value

    def project(first, count):
        rows = count * inner
        parts = [None] * (width // LANES)
        for j in range(group):
            for g in range(blocks):
                at = slice(g * points, (g + 1) * points)
                value = vj[j, :, at][None] * nfull[first : first + count, at][:, None, :]
                gbuf[:rows, at] = value.reshape(rows, points).astype(jnp.bfloat16)
            result = dot_t(gbuf[:rows], pad[top - offsets[j] : top - offsets[j] + length, :])
            for i in range(length // LANES):
                tile = starts[j] // LANES + i
                piece = result[:, i * LANES : (i + 1) * LANES]
                parts[tile] = piece if parts[tile] is None else parts[tile] + piece
        return jnp.concatenate(parts, axis=1)

    def apply(current, first, count):
        rows = slice(first * inner, (first + count) * inner)
        value = current[rows, :].astype(jnp.float32)
        scaled = (value.reshape(count, inner, width) * (gap[...] - CENTER)[None]).reshape(count * inner, width)
        return (scaled + project(first, count)) * (1.0 / HALF)

    screen()
    t1[...] = apply(amp, 0, vecs).astype(jnp.bfloat16)

    @pl.loop(0, blocks)
    def _(slot):
        expand(t1, slot)

    screen()
    pending = []
    first = 0
    for i, count in enumerate(chunks):
        rows = slice(first * inner, (first + count) * inner)
        size = count * inner
        value = 2.0 * apply(t1, first, count) - amp[rows, :].astype(jnp.float32)
        out[me, rows, :] = value.astype(jnp.bfloat16)
        copies = []
        for d in range(1, n_row):
            copy = remote(
                out.at[me, pl.ds(first * inner, size)], out.at[me, pl.ds(first * inner, size)],
                g_s.at[i, d - 1], g_r.at[i, d - 1], to(lax.rem(row + d, n_row), col),
            )
            copy.start()
            copies.append(copy)
        pending.append((first * inner, size, copies))
        first += count
    handed = []
    for i, (start, size, copies) in enumerate(pending):
        for d in range(n_row):
            if d > 0:
                copies[d - 1].wait_recv()
            slot = lax.rem(row + n_row - d, n_row) * n_col + col
            for e in range(1, n_col):
                copy = remote(
                    out.at[slot, pl.ds(start, size)], out.at[slot, pl.ds(start, size)],
                    h_s.at[i, e - 1, d], h_r.at[i, e - 1, d], to(row, lax.rem(col + e, n_col)),
                )
                copy.start()
                handed.append(copy)
    for copy in handed:
        copy.wait()
    for _, _, copies in pending:
        for copy in copies:
            copy.wait_send()


def on_device(sizes, amplitudes, pairs, stored_k, orbitals, valence_energy, conduction_energy, screened):
    n_pb, n_row, n_col = sizes
    _, vectors, pair_count, flat = amplitudes.shape
    count_v, count_c = valence_energy.shape[1], conduction_energy.shape[1]
    points = orbitals.shape[2]
    bands = orbitals.shape[1]
    blocks = n_row * n_col
    assert pair_count == n_row and vectors % n_col == 0 and count_v + count_c == bands
    vecs = vectors // n_col
    group, width, length, starts, offsets = windows(count_c)
    inner = count_v // group
    top = max(offsets)
    rows = vecs * inner
    rows_pad = -(-vecs // 16) * 16
    step = max(1, 16 // math.gcd(inner, 16))
    chunks, left = [], vecs
    while left > 0:
        chunks.append(min(left, 2 * step))
        left -= chunks[-1]
    row, col = lax.axis_index("row"), lax.axis_index("col")
    own = lax.dynamic_slice(amplitudes[0], (col * vecs, row, 0), (vecs, 1, flat)).reshape(rows, width)
    ev = jnp.repeat(valence_energy.reshape(-1, inner, group), count_c, axis=2)
    ec = jnp.tile(conduction_energy, (1, group))[:, None, :]
    dma = pltpu.SemaphoreType.DMA
    bf16, f32 = jnp.bfloat16, jnp.float32
    kc = len(chunks)
    smem, vmem = pl.BlockSpec(memory_space=pltpu.SMEM), pl.BlockSpec(memory_space=pltpu.VMEM)
    gathered = pl.pallas_call(
        functools.partial(kernel, (n_pb, n_row, n_col, count_v, count_c, vecs, points, chunks)),
        out_shape=jax.ShapeDtypeStruct((blocks, rows, width), bf16),
        in_specs=[smem, smem, vmem, vmem, vmem, vmem, vmem],
        out_specs=vmem,
        scratch_shapes=[
            pltpu.VMEM((n_pb, bands, points), bf16),
            pltpu.VMEM((n_row, bands, points), bf16),
            pltpu.VMEM((blocks, bands, points), bf16),
            pltpu.VMEM((points // LANES, count_v, LANES), f32),
            pltpu.VMEM((group, inner, blocks * points), f32),
            pltpu.VMEM((top + length, blocks * points), bf16),
            pltpu.VMEM((blocks, rows_pad, points), bf16),
            pltpu.VMEM((blocks, blocks // n_col, rows_pad, points), bf16),
            pltpu.VMEM((blocks, rows_pad, n_col * points), bf16),
            pltpu.VMEM((blocks, rows_pad, n_col * points), bf16),
            pltpu.VMEM((rows_pad, blocks * points), f32),
            pltpu.VMEM((rows, blocks * points), bf16),
            pltpu.VMEM((inner, width), f32),
            pltpu.VMEM((rows, width), bf16),
            dma((max(1, n_pb - 1),)), dma((max(1, n_pb - 1),)), dma,
            dma((n_row,)), dma((n_row,)),
            dma((n_col, n_row)), dma((n_col, n_row)),
            dma((blocks,)), dma((blocks,)),
            dma((blocks,)), dma((blocks,)),
            dma((kc, n_row)), dma((kc, n_row)),
            dma((kc, n_col, n_row)), dma((kc, n_col, n_row)),
        ],
        compiler_params=pltpu.CompilerParams(
            collective_id=0, has_side_effects=True, vmem_limit_bytes=48 * 1024 * 1024
        ),
    )(pairs[0], stored_k, own, orbitals[0], ev, ec, screened[0])
    spread = gathered.reshape(pair_count, vectors, flat)
    return jnp.transpose(spread, (1, 0, 2))[None]


def solution(mesh):
    sizes = (mesh.shape["pb"], mesh.shape["row"], mesh.shape["col"])
    return jax.shard_map(
        functools.partial(on_device, sizes),
        mesh=mesh,
        in_specs=(
            P("pb", None, None, None),
            P("pb", None, None),
            P(),
            P("pb", None, ("row", "col")),
            P(),
            P(),
            P("pb", "row", "col"),
        ),
        out_specs=P("pb", None, None, None),
        check_vma=False,
    )
```
